512 devices in a mesh: table: 16 (over x, y), replica: 32 (over z, core).
Axes of the slice: x: 4, y: 4, z: 16, core: 2. Of those that a mesh axis runs over, the one named last changes fastest.
Arguments:
- embeds: bfloat16 [131072, 512], P('replica', 'table'), may hold values from -6 to 6
- cotangent: bfloat16 [131072, 512], P('replica', 'table'), may hold values from -6 to 6
- send_plan: int32 [32, 16, 32], P('replica'), may hold values from 0 to 31, each once within a row
- work_plan: int32 [32, 16, 32], P('replica', 'table'), may hold values from 0 to 31, each once within a row
- sequence_tiles: int32 [32, 16, 4], P('replica', 'table'), may hold values from 1 to 16, 32 in all within a row
- slopes: float32 [8], replicated, may hold values from 0.002 to 0.2
- uvqk_weight: bfloat16 [512, 2048], replicated, may hold values from -0.25 to 0.25
- out_weight: bfloat16 [512, 512], replicated, may hold values from -0.25 to 0.25
Outputs:
- layer_output: bfloat16 [131072, 512], P('replica', 'table')
- input_gradient: bfloat16 [131072, 512], P('replica', 'table')
The draws below stay inside these ranges and needn't reach their ends.
Inputs may be any that keep to these rules, and one draw needn't show every extreme that they name: `send_plan`: a device's 32 entries are all different. `work_plan`: a device's 32 entries are all different. `sequence_tiles`: a device's 4 entries sum to 32.
All inputs are finite; a program needn't handle non-finite values.
Results may differ from the reference program's by a relative error of at most 0.013.
Values may be sent and summed in bfloat16 or wider, within the bound.
No kernel may reach another device: no remote copies, remote signals or barrier semaphores. Data moves between devices by JAX's collectives and lax.ppermute only.
A program may use at most 64 MiB of HBM per device.

```python
import math
import jax
import jax.numpy as jnp
import numpy as np
from jax import lax

D = 512
HEADS = 8
TILE = 8
PEER_TILES = 1
SEQ_DEV = 4
TILES_DEV = 32
TOK_DEV = 256
REPLICAS = 32
TABLES = 16
TOKENS = 131072
N_TABLE = 16
N_REPLICA = 32


def level_of(own_key, extent, cuts, least, high):
    gain = 1.0
    for dim, blocks in cuts:
        draws = jax.random.uniform(jax.random.fold_in(jax.random.fold_in(own_key, 6), dim), (blocks,), jnp.float32, least / len(cuts), high / len(cuts))
        gain = gain * jnp.repeat(jnp.exp(draws), extent[dim] // blocks).reshape((-1,) + (1,) * (len(extent) - 1 - dim))
    return gain


def length_profile(amount, total, bound, slope):
    portions = [(1 << 20) // math.isqrt(standing ** slope) + 1 for standing in range(2, amount + 1)]
    rest, holding = total - bound - (amount - 1), [1] * (amount - 1)
    while rest > 0:
        movable = [i for i in range(amount - 1) if holding[i] < bound]
        mass, remaining = sum([portions[i] for i in movable]), rest
        for i in movable:
            more = min(bound - holding[i], max(1, remaining * portions[i] // mass), rest)
            holding[i] = holding[i] + more
            rest = rest - more
    return np.array([bound] + holding)


def ragged_sizes(key, amount, total, limit, slope):
    if amount == 2:
        one = jax.random.randint(key, (), max(1, total - limit), min(limit, total - 1) + 1)
        return jnp.stack([one, total - one])
    tallies = jnp.asarray(length_profile(amount, total, limit, slope), jnp.int32)
    couples = (amount - 1) // 2
    donor, receiver = tallies[1:1 + 2 * couples:2], tallies[2:2 + 2 * couples:2]
    slack = jnp.minimum(donor - 1, limit - receiver)
    passed = jax.random.randint(jax.random.fold_in(key, 1), (couples,), 0, 1 << 20) % (slack + 1)
    tallies = tallies.at[1:1 + 2 * couples:2].set(donor - passed).at[2:2 + 2 * couples:2].set(receiver + passed)
    return tallies[jax.random.permutation(jax.random.fold_in(key, 2), amount)]


def noise(own_key, dims, width, bound, split=(), held_as=jnp.bfloat16):
    factor_of = level_of(own_key, dims, split, -0.22, 0.18) if split else 1.0
    array = jax.random.normal(own_key, dims, jnp.float32) * width * factor_of
    return jnp.minimum(jnp.maximum(array, -bound), bound).astype(held_as)


def setup_inputs(seed: int = 0) -> dict:
    splits = jax.random.split(jax.random.key(seed), 9)
    return {
        "embeds": noise(splits[0], (TOKENS, D), 1.0, 6.0, ((0, 32), (1, 16))),
        "cotangent": noise(splits[1], (TOKENS, D), 1.0, 6.0, ((0, 32), (1, 16))),
        "send_plan": jax.vmap(lambda own: jax.random.permutation(own, TILES_DEV))(jax.random.split(splits[2], REPLICAS * TABLES)).reshape((REPLICAS, TABLES, TILES_DEV)).astype(jnp.int32),
        "work_plan": jax.vmap(lambda own: jax.random.permutation(own, TILES_DEV))(jax.random.split(splits[3], REPLICAS * TABLES)).reshape((REPLICAS, TABLES, TILES_DEV)).astype(jnp.int32),
        "sequence_tiles": jax.vmap(lambda own: ragged_sizes(own, SEQ_DEV, TILES_DEV, TILES_DEV // 2, 2))(jax.random.split(splits[4], REPLICAS * TABLES)).reshape((REPLICAS, TABLES, SEQ_DEV)).astype(jnp.int32),
        "slopes": jnp.clip(jnp.exp(jax.random.uniform(splits[5], (HEADS,), jnp.float32, math.log(0.002), math.log(0.2))), 0.002, 0.2),
        "uvqk_weight": noise(splits[6], (D, 4 * D), D ** -0.5, 0.25),
        "out_weight": noise(splits[7], (D, D), D ** -0.5, 0.25),
    }


EPSILON = 1e-05

def layer_norm(features):
    centre = lax.optimization_barrier(jnp.mean(features, axis=-1, keepdims=True))
    centred = features - centre
    spread = lax.optimization_barrier(jnp.mean(centred * centred, axis=-1, keepdims=True))
    return centred * lax.rsqrt(spread + EPSILON)

def segment_ids(lengths, row_count, tile_rows):
    boundary = jnp.cumsum(lengths.astype(jnp.int32))
    tile_index = jnp.arange(row_count, dtype=jnp.int32) // tile_rows
    return lax.optimization_barrier(jnp.sum((tile_index[None, :] >= boundary[:, None]).astype(jnp.int32), axis=0))

def hstu_layer(inputs, segment, slopes, uvqk_weight, out_weight):
    row_count, feature_count = inputs.shape
    head_count = slopes.shape[0]
    head_size = feature_count // head_count
    score_scale = head_size ** (-0.5)
    normed = layer_norm(inputs.astype(jnp.float32)).astype(jnp.bfloat16)
    projected = jax.nn.silu(jnp.dot(normed, uvqk_weight, preferred_element_type=jnp.float32))
    gate_part = projected[:, :feature_count]
    value_part = projected[:, feature_count:2 * feature_count].astype(jnp.bfloat16)
    query_part = projected[:, 2 * feature_count:3 * feature_count].astype(jnp.bfloat16)
    key_part = projected[:, 3 * feature_count:].astype(jnp.bfloat16)
    row_index = lax.broadcasted_iota(jnp.int32, (row_count, row_count), 0)
    col_index = lax.broadcasted_iota(jnp.int32, (row_count, row_count), 1)
    allowed = (segment[:, None] == segment[None, :]) & (col_index <= row_index)
    distance = (row_index - col_index).astype(jnp.float32)
    pieces = []
    for head_index in range(head_count):
        lower = head_index * head_size
        upper = lower + head_size
        scores = jnp.dot(query_part[:, lower:upper], key_part[:, lower:upper].T, preferred_element_type=jnp.float32)
        scores = scores * score_scale - slopes[head_index] * distance
        weights = jnp.where(allowed, jax.nn.silu(scores), jnp.zeros_like(scores)).astype(jnp.bfloat16)
        pieces.append(jnp.dot(weights, value_part[:, lower:upper], preferred_element_type=jnp.float32))
    attended = jnp.concatenate(pieces, axis=1)
    gated = (layer_norm(attended) * gate_part).astype(jnp.bfloat16)
    mixing = jnp.dot(gated, out_weight, preferred_element_type=jnp.float32)
    return (inputs.astype(jnp.float32) + mixing).astype(jnp.bfloat16)

def forward_backward(inputs, grad_rows, segment, slopes, uvqk_weight, out_weight):

    def apply_layer(layer_input):
        return hstu_layer(layer_input, segment, slopes, uvqk_weight, out_weight)
    outputs, pullback = jax.vjp(apply_layer, inputs)
    return (outputs, pullback(grad_rows)[0])

def reference(embeds, cotangent, send_plan, work_plan, sequence_tiles, slopes, uvqk_weight, out_weight):
    table_count = N_TABLE
    replica_count = N_REPLICA
    device_count = replica_count * table_count
    dest_index = jnp.arange(replica_count, dtype=jnp.int32)[:, None, None]
    table_index = jnp.arange(table_count, dtype=jnp.int32)[None, :, None]
    source_index = (work_plan // PEER_TILES).astype(jnp.int32)
    place_index = (work_plan % PEER_TILES).astype(jnp.int32)
    home_tile = send_plan[source_index, table_index, dest_index * PEER_TILES + place_index].astype(jnp.int32)
    flat_index = ((source_index * table_count + table_index) * TILES_DEV + home_tile).reshape(-1).astype(jnp.int32)
    home_inputs = embeds.reshape(-1, TILE, D)
    home_grads = cotangent.reshape(-1, TILE, D)
    work_inputs = home_inputs[flat_index].reshape(device_count, TOK_DEV, D)
    work_grads = home_grads[flat_index].reshape(device_count, TOK_DEV, D)
    lengths = sequence_tiles.reshape(device_count, SEQ_DEV)

    def one_device(packed):
        inputs, grad_rows, counts = packed
        segment = segment_ids(counts, TOK_DEV, TILE)
        return forward_backward(inputs, grad_rows, segment, slopes, uvqk_weight, out_weight)
    outputs, gradient = lax.map(one_device, (work_inputs, work_grads, lengths))
    layer_output = jnp.zeros_like(home_inputs).at[flat_index].set(outputs.reshape(-1, TILE, D)).reshape(embeds.shape)
    input_gradient = jnp.zeros_like(home_grads).at[flat_index].set(gradient.reshape(-1, TILE, D)).reshape(embeds.shape)
    return (layer_output, input_gradient)
```

```python
import jax
import jax.numpy as jnp
from jax import lax
from jax.experimental import pallas as pl
from jax.experimental.pallas import tpu as pltpu
from jax.sharding import PartitionSpec as P

TILE = 8
HALF = 4
EPSILON = 1e-05
BF16 = jnp.bfloat16
F32 = jnp.float32
FAR = 1e30


def dot(a, b, ca=1, cb=0):
    return lax.dot_general(a, b, (((ca,), (cb,)), ((), ())), preferred_element_type=F32)


def one_hot(rows, target):
    index = lax.broadcasted_iota(jnp.int32, (rows, target.shape[1]), 0)
    return jnp.where(index == target, 1.0, 0.0).astype(BF16)


def spread(plan, repeat):
    slots = plan.shape[1]
    lanes = slots * repeat
    slot = lax.broadcasted_iota(jnp.int32, (slots, lanes), 0)
    lane = lax.broadcasted_iota(jnp.int32, (slots, lanes), 1)
    pick = jnp.where(lane // repeat == slot, 1.0, 0.0).astype(BF16)
    return dot(plan.astype(F32).astype(BF16), pick).astype(jnp.int32)


def lane_index(lanes):
    return lax.broadcasted_iota(jnp.int32, (1, lanes), 1)


def to_blocks(top, bottom):
    m = top.shape[1] // 2
    return jnp.concatenate([top[:, :m], bottom[:, :m], top[:, m:], bottom[:, m:]], axis=0).T


def from_blocks(block):
    turned = block.T
    c2 = turned.shape[0] // 2
    return jnp.concatenate([turned[:c2], turned[c2:]], axis=1)


def send_kernel(plan_ref, x_ref, g_ref, out_ref):
    tables, peers = plan_ref.shape
    rows = peers * TILE
    m = peers * HALF
    lane = lane_index(m)
    base = spread(plan_ref[...], HALF) * TILE + lane % HALF
    target = jnp.concatenate([base, base + HALF], axis=1)
    for t in range(tables):
        pick = one_hot(rows, target[t : t + 1])
        span = pl.ds(t * rows, rows)
        top = dot(x_ref[:, span], pick).astype(BF16)
        bottom = dot(g_ref[:, span], pick).astype(BF16)
        out_ref[pl.ds(t * m, m), :] = to_blocks(top, bottom)


def home_kernel(back_ref, in_ref, y_ref, d_ref):
    tables, peers = back_ref.shape
    rows = peers * TILE
    m = peers * HALF
    lane = lane_index(rows)
    inner = lane % TILE
    target = spread(back_ref[...], TILE) * HALF + inner % HALF + (inner // HALF) * m
    c = y_ref.shape[0]
    for t in range(tables):
        place = one_hot(2 * m, target[t : t + 1])
        span = pl.ds(t * rows, rows)
        got = dot(from_blocks(in_ref[pl.ds(t * m, m), :]), place).astype(BF16)
        y_ref[:, span] = got[:c]
        d_ref[:, span] = got[c:]


def norm_parts(x):
    n = x.shape[0]
    centred = x - jnp.sum(x, axis=0, keepdims=True) * (1.0 / n)
    spread_ = jnp.sum(centred * centred, axis=0, keepdims=True) * (1.0 / n)
    inv = lax.rsqrt(spread_ + EPSILON)
    return centred * inv, inv


def norm_back(grad, normed, inv):
    n = grad.shape[0]
    mean = jnp.sum(grad, axis=0, keepdims=True) * (1.0 / n)
    along = jnp.sum(grad * normed, axis=0, keepdims=True) * (1.0 / n)
    return inv * (grad - mean - normed * along)


def layer_kernel(
    slopes_ref, in_ref, pick_ref, place_ref, far_ref, wt_ref, w_ref, ot_ref, o_ref, out_ref,
    x_ref, g_ref, slope_ref, gate_ref, v_ref, q_ref, k_ref, w8_ref, d8_ref, att_ref, dp_ref,
    y_ref, dx_ref,
):
    features, rows = x_ref.shape
    heads = slopes_ref.shape[0]
    size = features // heads
    tables = in_ref.shape[0] // (rows // 2)
    m = rows // 2
    c = features // tables
    for t in range(tables):
        both = from_blocks(in_ref[pl.ds(t * m, m), :])
        x_ref[pl.ds(t * c, c), :] = both[:c]
        g_ref[pl.ds(t * c, c), :] = both[c:]
    pick = pick_ref[...]
    x = dot(x_ref[...], pick)
    g = dot(g_ref[...], pick)
    x_ref[...] = x.astype(BF16)
    g_ref[...] = g.astype(BF16)
    normed, inv = norm_parts(x)
    sent = normed.astype(BF16)

    step = 256
    scale = size ** (-0.5)
    for part in range(0, 4 * features, step):
        half = dot(wt_ref[pl.ds(part, step), :], sent)
        bend = jnp.tanh(half)
        act = half + half * bend
        slope_ref[pl.ds(part, step), :] = (1.0 + bend) * (1.0 + half * (1.0 - bend))
        at = pl.ds(part % features, step)
        kind = part // features
        if kind == 0:
            gate_ref[at, :] = act
        elif kind == 1:
            v_ref[at, :] = act.astype(BF16)
        elif kind == 2:
            q_ref[at, :] = (act * (scale * 0.5)).astype(BF16)
        else:
            k_ref[at, :] = act.astype(BF16)

    row = lax.broadcasted_iota(jnp.int32, (m, rows), 0)
    col = lax.broadcasted_iota(jnp.int32, (m, rows), 1)
    apart = (col - row).astype(F32)
    for h in range(heads):
        at = pl.ds(h * size, size)
        slope = slopes_ref[h] * 0.5
        for b in range(2):
            keys = pl.ds(b * m, m)
            asks = pl.ds(b * m, rows - b * m)
            dist = apart[:, : rows - b * m]
            half = dot(k_ref[at, keys], q_ref[at, asks], 0, 0)
            half = (half - far_ref[keys, asks]) - slope * dist
            bend = jnp.tanh(half)
            w8_ref[h, keys, asks] = (half + half * bend).astype(BF16)
            d8_ref[h, keys, asks] = (1.0 + bend) * (1.0 + half * (1.0 - bend))
        low = dot(v_ref[at, :], w8_ref[h, :, pl.ds(m, m)])
        att_ref[at, pl.ds(m, m)] = low
        att_ref[at, pl.ds(0, m)] = dot(v_ref[at, pl.ds(0, m)], w8_ref[h, pl.ds(0, m), pl.ds(0, m)])

    gate = gate_ref[...]
    even, inv_a = norm_parts(att_ref[...])
    gated = (even * gate).astype(BF16)
    y_ref[...] = (x_ref[...].astype(F32) + dot(ot_ref[...], gated)).astype(BF16)

    d_gated = dot(o_ref[...], g_ref[...]).astype(BF16).astype(F32)
    dp_ref[pl.ds(0, features), :] = (d_gated * even * slope_ref[pl.ds(0, features), :]).astype(BF16)
    att_ref[...] = norm_back(d_gated * gate, even, inv_a)
    for h in range(heads):
        at = pl.ds(h * size, size)
        d_att = att_ref[at, :].astype(BF16)
        v = v_ref[at, :]
        k = k_ref[at, :]
        q = q_ref[at, :]
        top = dot(v[:, :m], d_att, 0, 0) * d8_ref[h, pl.ds(0, m), :]
        low = dot(v[:, m:], d_att[:, m:], 0, 0) * d8_ref[h, pl.ds(m, m), pl.ds(m, m)]
        top = top.astype(BF16)
        low = low.astype(BF16)
        dv0 = dot(d_att, w8_ref[h, pl.ds(0, m), :], 1, 1)
        dv1 = dot(d_att[:, m:], w8_ref[h, pl.ds(m, m), pl.ds(m, m)], 1, 1)
        dk0 = dot(q, top, 1, 1)
        dk1 = dot(q[:, m:], low, 1, 1)
        dq0 = dot(k[:, :m], top[:, :m])
        dq1 = dot(k, jnp.concatenate([top[:, m:], low], axis=0))
        for kind, grad in (
            (1, jnp.concatenate([dv0, dv1], axis=1)),
            (2, jnp.concatenate([dq0, dq1], axis=1) * (scale * 0.5)),
            (3, jnp.concatenate([dk0, dk1], axis=1)),
        ):
            to = pl.ds(kind * features + h * size, size)
            dp_ref[to, :] = (grad * slope_ref[to, :]).astype(BF16)

    d_normed = (dot(w_ref[...], dp_ref[...]) * 0.5).astype(BF16).astype(F32)
    normed, inv = norm_parts(x_ref[...].astype(F32))
    back = norm_back(d_normed, normed, inv).astype(BF16).astype(F32)
    dx_ref[...] = (back + g_ref[...].astype(F32)).astype(BF16)

    place = place_ref[...]
    y_ref[...] = dot(y_ref[...], place).astype(BF16)
    dx_ref[...] = dot(dx_ref[...], place).astype(BF16)
    for t in range(tables):
        at = pl.ds(t * c, c)
        out_ref[pl.ds(t * m, m), :] = to_blocks(y_ref[at, :], dx_ref[at, :])


def vmem(n):
    return [pl.BlockSpec(memory_space=pltpu.VMEM)] * n


def inverse(plan):
    n = plan.shape[-1]
    index = jnp.arange(n, dtype=jnp.int32)
    hit = plan[..., :, None] == index
    return jnp.sum(jnp.where(hit, index[:, None], 0), axis=-2)


def layer(blocks, pick, place, far, slopes, uvqk_weight, out_weight):
    features = uvqk_weight.shape[0]
    heads = slopes.shape[0]
    rows = pick.shape[0]
    wide = pltpu.VMEM((features, rows), F32)
    thin = pltpu.VMEM((features, rows), BF16)
    return pl.pallas_call(
        layer_kernel,
        out_shape=jax.ShapeDtypeStruct(blocks.shape, BF16),
        in_specs=[pl.BlockSpec(memory_space=pltpu.SMEM)] + vmem(8),
        out_specs=pl.BlockSpec(memory_space=pltpu.VMEM),
        scratch_shapes=[
            thin, thin, pltpu.VMEM((4 * features, rows), F32), wide, thin, thin, thin,
            pltpu.VMEM((heads, rows, rows), BF16), pltpu.VMEM((heads, rows, rows), F32),
            wide, pltpu.VMEM((4 * features, rows), BF16), thin, thin,
        ],
        name="layer",
    )(
        slopes, blocks, pick, place, far,
        (uvqk_weight * jnp.asarray(0.5, BF16)).T, uvqk_weight, out_weight.T, out_weight,
    )


def tables_of(own_work, lengths, rows):
    peers = rows // TILE
    m = peers * HALF
    lane = jnp.arange(rows, dtype=jnp.int32)
    inner = lane % TILE
    spot = jnp.repeat(own_work, TILE) * HALF + inner % HALF + (inner // HALF) * m
    pick = (lane[:, None] == spot[None, :]).astype(BF16)
    place = (spot[:, None] == lane[None, :]).astype(BF16)
    bound = jnp.cumsum(lengths)
    segment = jnp.sum(((lane // TILE)[None, :] >= bound[:, None]).astype(jnp.int32), axis=0)
    seen = (segment[:, None] == segment[None, :]) & (lane[:, None] <= lane[None, :])
    return pick, place, jnp.where(seen, 0.0, FAR).astype(F32)


def shards(
    embeds, cotangent, send_plan, work_plan, sequence_tiles, slopes, uvqk_weight, out_weight
):
    tables = lax.axis_size("table")
    peers = lax.axis_size("replica")
    columns = embeds.shape[1]
    rows = embeds.shape[0] // tables
    plan = send_plan[0]
    sent = jax.ShapeDtypeStruct((tables * peers * HALF, 4 * columns), BF16)
    axes = ("table", "replica")
    blocks = pl.pallas_call(
        send_kernel, out_shape=sent, in_specs=vmem(3),
        out_specs=pl.BlockSpec(memory_space=pltpu.VMEM), name="send",
    )(plan, embeds.T, cotangent.T)

    def exchange(a):
        a = a.reshape(tables * peers, HALF, 4 * columns)
        a = lax.all_to_all(a, axes, split_axis=0, concat_axis=0, tiled=True)
        return a.reshape(sent.shape)

    pick, place, far = tables_of(work_plan[0, 0], sequence_tiles[0, 0], rows)
    done = layer(exchange(blocks), pick, place, far, slopes, uvqk_weight, out_weight)
    home = jax.ShapeDtypeStruct((columns, tables * rows), BF16)
    y, d = pl.pallas_call(
        home_kernel, out_shape=(home, home), in_specs=vmem(2),
        out_specs=(pl.BlockSpec(memory_space=pltpu.VMEM),) * 2, name="home",
    )(inverse(plan), exchange(done))
    return y.T, d.T


def solution(mesh):
    in_specs = (
        P("replica", "table"),
        P("replica", "table"),
        P("replica", None, None),
        P("replica", "table", None),
        P("replica", "table", None),
        P(),
        P(),
        P(),
    )
    out_specs = (P("replica", "table"), P("replica", "table"))
    return jax.shard_map(shards, mesh=mesh, in_specs=in_specs, out_specs=out_specs, check_vma=False)
```

```python
import jax
import jax.numpy as jnp
from jax import lax
from jax.experimental import pallas as pl
from jax.experimental.pallas import tpu as pltpu
from jax.sharding import PartitionSpec as P

TILE = 8
HALF = 4
EPSILON = 1e-05
BF16 = jnp.bfloat16
F32 = jnp.float32
FAR = 1e30
STEP = 128
PIECES = 2
GS, GP, GL, GH = 2200, 3500, 16000, 50000
FLAGS = None


def dot(a, b, ca=1, cb=0):
    return lax.dot_general(a, b, (((ca,), (cb,)), ((), ())), preferred_element_type=F32)


def one_hot(rows, target):
    index = lax.broadcasted_iota(jnp.int32, (rows, target.shape[1]), 0)
    return jnp.where(index == target, 1.0, 0.0).astype(BF16)


def spread(plan, repeat):
    slots = plan.shape[1]
    lanes = slots * repeat
    slot = lax.broadcasted_iota(jnp.int32, (slots, lanes), 0)
    lane = lax.broadcasted_iota(jnp.int32, (slots, lanes), 1)
    pick = jnp.where(lane // repeat == slot, 1.0, 0.0).astype(BF16)
    return dot(plan.astype(F32).astype(BF16), pick).astype(jnp.int32)


def spots(plan):
    rows = plan.shape[1] * TILE
    inner = lax.broadcasted_iota(jnp.int32, (1, rows), 1) % TILE
    return spread(plan, TILE) * HALF + inner % HALF + (inner // HALF) * (rows // 2)


def to_blocks(top, bottom):
    m = top.shape[1] // 2
    return jnp.concatenate([top[:, :m], bottom[:, :m], top[:, m:], bottom[:, m:]], axis=0).T


def from_blocks(block):
    turned = block.T
    c2 = turned.shape[0] // 2
    return jnp.concatenate([turned[:c2], turned[c2:]], axis=1)


def send_kernel(plan_ref, x_ref, g_ref, out_hbm, out_ref, out_sem):
    tables, peers = plan_ref.shape
    rows = peers * TILE
    m = peers * HALF
    per = tables // PIECES

    def leaving(i):
        span = pl.ds(i * per * m, per * m)
        return pltpu.make_async_copy(out_ref.at[span, :], out_hbm.at[span, :], out_sem.at[i])

    lane = lax.broadcasted_iota(jnp.int32, (1, m), 1)
    base = spread(plan_ref[...], HALF) * TILE + lane % HALF
    target = jnp.concatenate([base, base + HALF], axis=1)
    for i in range(PIECES):
        for t in range(i * per, (i + 1) * per):
            pick = one_hot(rows, target[t : t + 1])
            span = pl.ds(t * rows, rows)
            top = dot(x_ref[:, span], pick).astype(BF16)
            bottom = dot(g_ref[:, span], pick).astype(BF16)
            out_ref[pl.ds(t * m, m), :] = to_blocks(top, bottom)
        leaving(i).start()
    for i in range(PIECES):
        leaving(i).wait()


def home_kernel(back_ref, in_ref, y_hbm, d_hbm, y_ref, d_ref, out_sem):
    tables, peers = back_ref.shape
    rows = peers * TILE
    m = peers * HALF
    per = tables // PIECES
    target = spots(back_ref[...])
    c = y_ref.shape[0]

    def leaving(i):
        span = pl.ds(i * per * rows, per * rows)
        return [
            pltpu.make_async_copy(src.at[:, span], dst.at[:, span], out_sem.at[j, i])
            for j, (src, dst) in enumerate(((y_ref, y_hbm), (d_ref, d_hbm)))
        ]

    for i in range(PIECES):
        for t in range(i * per, (i + 1) * per):
            place = one_hot(2 * m, target[t : t + 1])
            span = pl.ds(t * rows, rows)
            got = dot(from_blocks(in_ref[pl.ds(t * m, m), :]), place).astype(BF16)
            y_ref[:, span] = got[:c]
            d_ref[:, span] = got[c:]
        for copy in leaving(i):
            copy.start()
    for i in range(PIECES):
        for copy in leaving(i):
            copy.wait()


def fold(x):
    return jnp.sum(x.reshape(x.shape[0] // 8, 8, x.shape[1]), axis=0)


def mean(partial, n):
    return jnp.sum(partial, axis=0, keepdims=True) * (1.0 / n)


def prep_kernel(lengths_ref, plan_ref, pick_ref, far_ref):
    rows = far_ref.shape[0]
    pick_ref[...] = one_hot(rows, spots(plan_ref[...]))
    key = lax.broadcasted_iota(jnp.int32, (rows, rows), 0)
    ask = lax.broadcasted_iota(jnp.int32, (rows, rows), 1)
    seen = key <= ask
    bound = 0
    for j in range(lengths_ref.shape[0]):
        bound = bound + lengths_ref[j] * TILE
        seen = seen & ((key >= bound) == (ask >= bound))
    far_ref[...] = jnp.where(seen, 0.0, FAR)


def layer_kernel(
    slopes_ref, in_ref, pick_ref, far_ref, w_ref, o_hbm, out_hbm,
    x_ref, g_ref, n_ref, slope_ref, gate_ref, v_ref, q_ref, k_ref, w8_ref, d8_ref, att_ref,
    datt_ref, dp_ref, y_ref, dx_ref, wt_ref, ot_ref, o_ref, out_ref, in_sem, out_sem,
):
    features, rows = x_ref.shape
    heads = slopes_ref.shape[0]
    size = features // heads
    m = rows // 2
    tables = in_ref.shape[0] // m
    c = features // tables
    per = STEP // c
    chunks = [pl.ds(part, STEP) for part in range(0, features, STEP)]
    none = jnp.zeros((8, rows), F32)
    read = pltpu.make_async_copy(o_hbm, o_ref, in_sem)
    read.start()

    for t in range(tables):
        both = from_blocks(in_ref[pl.ds(t * m, m), :])
        x_ref[pl.ds(t * c, c), :] = both[:c]
        g_ref[pl.ds(t * c, c), :] = both[c:]
    pick = pick_ref[...]
    total = none
    for at in chunks:
        x = dot(x_ref[at, :], pick)
        x_ref[at, :] = x.astype(BF16)
        n_ref[at, :] = x
        total = total + fold(x)
        g_ref[at, :] = dot(g_ref[at, :], pick).astype(BF16)
    centre = mean(total, features)
    total = none
    for at in chunks:
        x = n_ref[at, :] - centre
        total = total + fold(x * x)
    inv = lax.rsqrt(mean(total, features) + EPSILON)
    for at in chunks:
        normed = (n_ref[at, :] - centre) * inv
        n_ref[at, :] = normed
        dx_ref[at, :] = (normed * 0.5).astype(BF16)

    scale = size ** (-0.5)
    for part in range(0, 4 * features, STEP):
        wt_ref[pl.ds(part, STEP), :] = w_ref[:, pl.ds(part, STEP)].T
    for part in range(0, 4 * features, STEP):
        half = dot(wt_ref[pl.ds(part, STEP), :], dx_ref[...])
        bend = jnp.tanh(half)
        act = half + half * bend
        slope_ref[pl.ds(part, STEP), :] = (1.0 + bend) * (1.0 + half * (1.0 - bend))
        at = pl.ds(part % features, STEP)
        kind = part // features
        if kind == 0:
            gate_ref[at, :] = act
        elif kind == 1:
            v_ref[at, :] = act.astype(BF16)
        elif kind == 2:
            q_ref[at, :] = (act * (scale * 0.5)).astype(BF16)
        else:
            k_ref[at, :] = act.astype(BF16)

    row = lax.broadcasted_iota(jnp.int32, (m, rows), 0)
    col = lax.broadcasted_iota(jnp.int32, (m, rows), 1)
    apart = (col - row).astype(F32)
    for h in range(heads):
        at = pl.ds(h * size, size)
        slope = slopes_ref[h] * 0.5
        for b in range(2):
            keys = pl.ds(b * m, m)
            asks = pl.ds(b * m, rows - b * m)
            dist = apart[:, : rows - b * m]
            half = dot(k_ref[at, keys], q_ref[at, asks], 0, 0)
            half = (half - far_ref[keys, asks]) - slope * dist
            bend = jnp.tanh(half)
            w8_ref[h, keys, asks] = (half + half * bend).astype(BF16)
            d8_ref[h, keys, asks] = (1.0 + bend) * (1.0 + half * (1.0 - bend))
        att_ref[at, pl.ds(0, m)] = dot(v_ref[at, pl.ds(0, m)], w8_ref[h, pl.ds(0, m), pl.ds(0, m)])
        att_ref[at, pl.ds(m, m)] = dot(v_ref[at, :], w8_ref[h, :, pl.ds(m, m)])

    read.wait()
    for at in chunks:
        ot_ref[at, :] = o_ref[:, at].T
    total = none
    for at in chunks:
        total = total + fold(att_ref[at, :])
    centre = mean(total, features)
    total = none
    for at in chunks:
        x = att_ref[at, :] - centre
        total = total + fold(x * x)
    inv_a = lax.rsqrt(mean(total, features) + EPSILON)
    total, along = none, none
    for at in chunks:
        even = (att_ref[at, :] - centre) * inv_a
        att_ref[at, :] = even
        gate = gate_ref[at, :]
        datt_ref[at, :] = (even * gate).astype(BF16)
        d_gated = dot(o_ref[at, :], g_ref[...]).astype(BF16).astype(F32)
        dp_ref[at, :] = (d_gated * even * slope_ref[at, :]).astype(BF16)
        grad = d_gated * gate
        gate_ref[at, :] = grad
        total = total + fold(grad)
        along = along + fold(grad * even)
    for at in chunks:
        y_ref[at, :] = (x_ref[at, :].astype(F32) + dot(ot_ref[at, :], datt_ref[...])).astype(BF16)
    total, along = mean(total, features), mean(along, features)
    for at in chunks:
        grad = inv_a * (gate_ref[at, :] - total - att_ref[at, :] * along)
        datt_ref[at, :] = grad.astype(BF16)

    for h in range(heads):
        at = pl.ds(h * size, size)
        d_att = datt_ref[at, :]
        v = v_ref[at, :]
        k = k_ref[at, :]
        q = q_ref[at, :]
        top = dot(v[:, :m], d_att, 0, 0) * d8_ref[h, pl.ds(0, m), :]
        low = dot(v[:, m:], d_att[:, m:], 0, 0) * d8_ref[h, pl.ds(m, m), pl.ds(m, m)]
        top = top.astype(BF16)
        low = low.astype(BF16)
        dv0 = dot(d_att, w8_ref[h, pl.ds(0, m), :], 1, 1)
        dv1 = dot(d_att[:, m:], w8_ref[h, pl.ds(m, m), pl.ds(m, m)], 1, 1)
        dk0 = dot(q, top, 1, 1)
        dk1 = dot(q[:, m:], low, 1, 1)
        dq0 = dot(k[:, :m], top[:, :m])
        dq1 = dot(k, jnp.concatenate([top[:, m:], low], axis=0))
        for kind, lanes, grad in (
            (1, pl.ds(0, m), dv0), (1, pl.ds(m, m), dv1),
            (2, pl.ds(0, m), dq0 * (scale * 0.5)), (2, pl.ds(m, m), dq1 * (scale * 0.5)),
            (3, pl.ds(0, m), dk0), (3, pl.ds(m, m), dk1),
        ):
            to = pl.ds(kind * features + h * size, size)
            dp_ref[to, lanes] = (grad * slope_ref[to, lanes]).astype(BF16)

    total, along = none, none
    for at in chunks:
        grad = (dot(w_ref[at, :], dp_ref[...]) * 0.5).astype(BF16).astype(F32)
        gate_ref[at, :] = grad
        total = total + fold(grad)
        along = along + fold(grad * n_ref[at, :])
    total, along = mean(total, features), mean(along, features)
    place = pick.T

    def leaving(i):
        span = pl.ds(i * per * m, per * m)
        return pltpu.make_async_copy(out_ref.at[span, :], out_hbm.at[span, :], out_sem.at[i])

    for i, at in enumerate(chunks):
        back = inv * (gate_ref[at, :] - total - n_ref[at, :] * along)
        back = back.astype(BF16).astype(F32) + g_ref[at, :].astype(F32)
        y = dot(y_ref[at, :], place).astype(BF16)
        d = dot(back.astype(BF16), place).astype(BF16)
        for j in range(per):
            own = slice(j * c, (j + 1) * c)
            out_ref[pl.ds((i * per + j) * m, m), :] = to_blocks(y[own], d[own])
        leaving(i).start()
    for i in range(len(chunks)):
        leaving(i).wait()


def vmem(n):
    return [pl.BlockSpec(memory_space=pltpu.VMEM)] * n


def smem():
    return pl.BlockSpec(memory_space=pltpu.SMEM)


def hbm(n):
    return [pl.BlockSpec(memory_space=pltpu.HBM)] * n


def grant(room, flags=None):
    return pltpu.CompilerParams(vmem_limit_bytes=(65472 - room) << 10, flags=flags)


def inverse(plan):
    n = plan.shape[-1]
    index = jnp.arange(n, dtype=jnp.int32)
    hit = plan[..., :, None] == index
    return jnp.sum(jnp.where(hit, index[:, None], 0), axis=-2)


def send(plan, x, g):
    tables, peers = plan.shape
    columns = x.shape[0]
    sent = (tables * peers * HALF, 4 * columns)
    return pl.pallas_call(
        send_kernel,
        out_shape=jax.ShapeDtypeStruct(sent, BF16),
        in_specs=vmem(3),
        out_specs=hbm(1)[0],
        scratch_shapes=[pltpu.VMEM(sent, BF16), pltpu.SemaphoreType.DMA((PIECES,))],
        name="send", compiler_params=grant(GS),
    )(plan, x, g)


def home(back, got, columns):
    tables, peers = back.shape
    shape = (columns, tables * peers * TILE)
    return pl.pallas_call(
        home_kernel,
        out_shape=(jax.ShapeDtypeStruct(shape, BF16),) * 2,
        in_specs=vmem(2),
        out_specs=tuple(hbm(2)),
        scratch_shapes=[
            pltpu.VMEM(shape, BF16), pltpu.VMEM(shape, BF16),
            pltpu.SemaphoreType.DMA((2, PIECES)),
        ],
        name="home", compiler_params=grant(GH),
    )(back, got)


def prep(lengths, plan):
    rows = plan.shape[1] * TILE
    square = (rows, rows)
    return pl.pallas_call(
        prep_kernel,
        out_shape=(jax.ShapeDtypeStruct(square, BF16), jax.ShapeDtypeStruct(square, F32)),
        in_specs=[smem()] + vmem(1),
        out_specs=tuple(vmem(2)),
        name="prep", compiler_params=grant(GP),
        cost_estimate=pl.CostEstimate(flops=10**7, bytes_accessed=10**6, transcendentals=0),
    )(lengths, plan)


def layer(blocks, ready, slopes, w, o):
    pick, far = ready
    features = o.shape[0]
    heads = slopes.shape[0]
    rows = pick.shape[0]
    wide = pltpu.VMEM((features, rows), F32)
    thin = pltpu.VMEM((features, rows), BF16)
    return pl.pallas_call(
        layer_kernel,
        out_shape=jax.ShapeDtypeStruct(blocks.shape, BF16),
        in_specs=[smem()] + vmem(4) + hbm(1),
        out_specs=hbm(1)[0],
        scratch_shapes=[
            thin, thin, wide, pltpu.VMEM((4 * features, rows), F32), wide, thin, thin, thin,
            pltpu.VMEM((heads, rows, rows), BF16), pltpu.VMEM((heads, rows, rows), F32),
            wide, thin, pltpu.VMEM((4 * features, rows), BF16), thin, thin,
            pltpu.VMEM(w.shape[::-1], BF16), pltpu.VMEM(o.shape, BF16), pltpu.VMEM(o.shape, BF16),
            pltpu.VMEM(blocks.shape, BF16),
            pltpu.SemaphoreType.DMA, pltpu.SemaphoreType.DMA((features // STEP,)),
        ],
        name="layer", compiler_params=grant(GL, FLAGS),
    )(slopes, blocks, pick, far, w, o)


def shards(
    embeds, cotangent, send_plan, work_plan, sequence_tiles, slopes, uvqk_weight, out_weight
):
    columns = embeds.shape[1]
    plan = send_plan[0]
    tables, peers = plan.shape

    def exchange(a):
        shape = a.shape
        a = a.reshape(tables * peers, HALF, 4 * columns)
        a = lax.all_to_all(a, ("table", "replica"), split_axis=0, concat_axis=0, tiled=True)
        return a.reshape(shape)

    got = exchange(send(plan, embeds.T, cotangent.T))
    ready = prep(sequence_tiles[0, 0], work_plan[0])
    done = layer(got, ready, slopes, uvqk_weight, out_weight)
    y, d = home(inverse(plan), exchange(done), columns)
    return y.T, d.T


def solution(mesh):
    in_specs = (
        P("replica", "table"),
        P("replica", "table"),
        P("replica", None, None),
        P("replica", "table", None),
        P("replica", "table", None),
        P(),
        P(),
        P(),
    )
    out_specs = (P("replica", "table"), P("replica", "table"))
    return jax.shard_map(shards, mesh=mesh, in_specs=in_specs, out_specs=out_specs, check_vma=False)
```

```python
import jax
import jax.numpy as jnp
from jax import lax
from jax.experimental import pallas as pl
from jax.experimental.pallas import tpu as pltpu
from jax.sharding import PartitionSpec as P

TILE = 8
HALF = 4
EPSILON = 1e-05
BF16 = jnp.bfloat16
F32 = jnp.float32
FAR = 1e30
STEP = 128
PIECES = 2
GS, GP, GL, GH = 2200, 0, 16000, 50000
F0S = None


def dot(a, b, ca=1, cb=0):
    return lax.dot_general(a, b, (((ca,), (cb,)), ((), ())), preferred_element_type=F32)


def one_hot(rows, target):
    index = lax.broadcasted_iota(jnp.int32, (rows, target.shape[1]), 0)
    return jnp.where(index == target, 1.0, 0.0).astype(BF16)


def spread(plan, repeat):
    slots = plan.shape[1]
    lanes = slots * repeat
    slot = lax.broadcasted_iota(jnp.int32, (slots, lanes), 0)
    lane = lax.broadcasted_iota(jnp.int32, (slots, lanes), 1)
    pick = jnp.where(lane // repeat == slot, 1.0, 0.0).astype(BF16)
    return dot(plan.astype(F32).astype(BF16), pick).astype(jnp.int32)


def spots(plan):
    rows = plan.shape[1] * TILE
    inner = lax.broadcasted_iota(jnp.int32, (1, rows), 1) % TILE
    return spread(plan, TILE) * HALF + inner % HALF + (inner // HALF) * (rows // 2)


def to_blocks(top, bottom):
    m = top.shape[1] // 2
    return jnp.concatenate([top[:, :m], bottom[:, :m], top[:, m:], bottom[:, m:]], axis=0).T


def from_blocks(block):
    turned = block.T
    c2 = turned.shape[0] // 2
    return jnp.concatenate([turned[:c2], turned[c2:]], axis=1)


def send_kernel(plan_ref, x_ref, g_ref, out_hbm, out_ref, out_sem):
    tables, peers = plan_ref.shape
    rows = peers * TILE
    m = peers * HALF
    per = tables // PIECES

    def leaving(i):
        span = pl.ds(i * per * m, per * m)
        return pltpu.make_async_copy(out_ref.at[span, :], out_hbm.at[span, :], out_sem.at[i])

    lane = lax.broadcasted_iota(jnp.int32, (1, m), 1)
    base = spread(plan_ref[...], HALF) * TILE + lane % HALF
    target = jnp.concatenate([base, base + HALF], axis=1)
    for i in range(PIECES):
        for t in range(i * per, (i + 1) * per):
            pick = one_hot(rows, target[t : t + 1])
            span = pl.ds(t * rows, rows)
            top = dot(x_ref[:, span], pick).astype(BF16)
            bottom = dot(g_ref[:, span], pick).astype(BF16)
            out_ref[pl.ds(t * m, m), :] = to_blocks(top, bottom)
        leaving(i).start()
    for i in range(PIECES):
        leaving(i).wait()


def home_kernel(back_ref, in_ref, y_hbm, d_hbm, y_ref, d_ref, out_sem):
    tables, peers = back_ref.shape
    rows = peers * TILE
    m = peers * HALF
    per = tables // PIECES
    target = spots(back_ref[...])
    c = y_ref.shape[0]

    def leaving(i):
        span = pl.ds(i * per * rows, per * rows)
        return [
            pltpu.make_async_copy(src.at[:, span], dst.at[:, span], out_sem.at[j, i])
            for j, (src, dst) in enumerate(((y_ref, y_hbm), (d_ref, d_hbm)))
        ]

    for i in range(PIECES):
        for t in range(i * per, (i + 1) * per):
            place = one_hot(2 * m, target[t : t + 1])
            span = pl.ds(t * rows, rows)
            got = dot(from_blocks(in_ref[pl.ds(t * m, m), :]), place).astype(BF16)
            y_ref[:, span] = got[:c]
            d_ref[:, span] = got[c:]
        for copy in leaving(i):
            copy.start()
    for i in range(PIECES):
        for copy in leaving(i):
            copy.wait()


def fold(x):
    return jnp.sum(x.reshape(x.shape[0] // 8, 8, x.shape[1]), axis=0)


def mean(partial, n):
    return jnp.sum(partial, axis=0, keepdims=True) * (1.0 / n)


def allowed(lengths_ref, rows):
    key = lax.broadcasted_iota(jnp.int32, (rows, rows // 2), 0)
    ask = lax.broadcasted_iota(jnp.int32, (1, rows), 1)
    key_of, ask_of, bound = jnp.zeros_like(key), jnp.zeros_like(ask), 0
    for j in range(lengths_ref.shape[0] - 1):
        bound = bound + lengths_ref[j] * TILE
        key_of = jnp.where(key >= bound, j + 1, key_of)
        ask_of = jnp.where(ask >= bound, j + 1, ask_of)
    key, key_of = (jnp.concatenate([a, a], axis=1) for a in (key, key_of))
    return jnp.where((key <= ask) & (key_of == ask_of), 0.0, FAR)


def activate(half):
    lift = 1.0 + jnp.tanh(half)
    act = half * lift
    return act, lift * (((half + half) - act) + 1.0)


def layer_kernel(
    slopes_ref, lengths_ref, plan_ref, in_ref, w_ref, o_hbm, out_hbm,
    far_ref, x_ref, g_ref, n_ref, slope_ref, gate_ref, v_ref, q_ref, k_ref, w8_ref, d8_ref, att_ref,
    s8_ref, datt_ref, dp_ref, y_ref, dx_ref, wt_ref, ot_ref, o_ref, out_ref, in_sem, out_sem,
):
    features, rows = x_ref.shape
    heads = slopes_ref.shape[0]
    size = features // heads
    m = rows // 2
    tables = in_ref.shape[0] // m
    c = features // tables
    per = STEP // c
    chunks = [pl.ds(part, STEP) for part in range(0, features, STEP)]
    none = jnp.zeros((8, rows), F32)
    first, last = pl.ds(0, m), pl.ds(m, m)
    zero = jnp.minimum(lengths_ref[0], 0)
    read = pltpu.make_async_copy(o_hbm, o_ref, in_sem)
    read.start()

    for t in range(tables):
        both = from_blocks(in_ref[pl.ds(t * m, m), :])
        x_ref[pl.ds(t * c, c), :] = both[:c]
        g_ref[pl.ds(t * c, c), :] = both[c:]
    pick = one_hot(rows, spots(plan_ref[...]))
    far_ref[...] = allowed(lengths_ref, rows)
    total = none
    for at in chunks:
        x = dot(x_ref[at, :], pick)
        x_ref[at, :] = x.astype(BF16)
        n_ref[at, :] = x
        total = total + fold(x)
        g_ref[at, :] = dot(g_ref[at, :], pick).astype(BF16)
    centre = mean(total, features)
    total = none
    for at in chunks:
        x = n_ref[at, :] - centre
        total = total + fold(x * x)
    inv = lax.rsqrt(mean(total, features) + EPSILON)
    for at in chunks:
        normed = (n_ref[at, :] - centre) * inv
        n_ref[at, :] = normed
        dx_ref[at, :] = (normed * 0.5).astype(BF16)

    scale = size ** (-0.5)
    for part in range(0, 4 * features, STEP):
        wt_ref[pl.ds(part, STEP), :] = w_ref[:, pl.ds(part, STEP)].T
    for part in range(0, 4 * features, STEP):
        half = dot(wt_ref[pl.ds(part, STEP), :], dx_ref[...])
        act, slope_ref[pl.ds(part, STEP), :] = activate(half)
        at = pl.ds(part % features, STEP)
        kind = part // features
        if kind == 0:
            gate_ref[at, :] = act
        elif kind == 1:
            v_ref[at, :] = act.astype(BF16)
        elif kind == 2:
            q_ref[at, :] = (act * (scale * 0.5)).astype(BF16)
        else:
            k_ref[at, :] = act.astype(BF16)

    row = lax.broadcasted_iota(jnp.int32, (m, rows), 0)
    col = lax.broadcasted_iota(jnp.int32, (m, rows), 1)
    apart = (col - row).astype(F32)
    for h in range(heads):
        at = pl.ds(h * size, size)
        slope = slopes_ref[h] * 0.5
        for b in range(2):
            keys = pl.ds(b * m, m)
            asks = pl.ds(b * m, rows - b * m)
            dist = apart[:, : rows - b * m]
            half = dot(k_ref[at, keys], q_ref[at, asks], 0, 0)
            half = (half - far_ref[keys, asks]) - slope * dist
            act, d8_ref[h, keys, asks] = activate(half)
            w8_ref[h, keys, asks] = act.astype(BF16)
    for h in range(heads):
        at = pl.ds(h * size, size)
        att_ref[at, pl.ds(0, m)] = dot(v_ref[at, pl.ds(0, m)], w8_ref[h, pl.ds(0, m), pl.ds(0, m)])
        att_ref[at, pl.ds(m, m)] = dot(v_ref[at, :], w8_ref[h, :, pl.ds(m, m)])

    read.wait()
    for at in chunks:
        ot_ref[at, :] = o_ref[:, at].T
    total = none
    for at in chunks:
        total = total + fold(att_ref[at, :])
    centre = mean(total, features)
    total = none
    for at in chunks:
        x = att_ref[at, :] - centre
        total = total + fold(x * x)
    inv_a = lax.rsqrt(mean(total, features) + EPSILON)
    total, along = none, none
    for at in chunks:
        even = (att_ref[at, :] - centre) * inv_a
        att_ref[at, :] = even
        gate = gate_ref[at, :]
        datt_ref[at, :] = (even * gate).astype(BF16)
        d_gated = dot(o_ref[at, :], g_ref[...]).astype(BF16).astype(F32)
        dp_ref[at, :] = (d_gated * even * slope_ref[at, :]).astype(BF16)
        grad = d_gated * gate
        gate_ref[at, :] = grad
        total = total + fold(grad)
        along = along + fold(grad * even)
    for at in chunks:
        y_ref[at, :] = (x_ref[at, :].astype(F32) + dot(ot_ref[at, :], datt_ref[...])).astype(BF16)
    total, along = mean(total, features), mean(along, features)
    for at in chunks:
        grad = inv_a * (gate_ref[at, :] - total - att_ref[at, :] * along)
        datt_ref[at, :] = grad.astype(BF16)

    for h in range(heads):
        at = pl.ds(h * size, size)
        top = dot(v_ref[at, first], datt_ref[at, :], 0, 0) * d8_ref[h + zero, first, :]
        s8_ref[h, first, :] = top.astype(BF16)
        low = dot(v_ref[at, last], datt_ref[at, last], 0, 0) * d8_ref[h + zero, last, last]
        s8_ref[h, last, last] = low.astype(BF16)
    for h in range(heads):
        at = pl.ds(h * size, size)
        lag = h + 0
        for kind, lanes, grad in (
            (1, first, dot(datt_ref[at, :], w8_ref[lag, first, :], 1, 1)),
            (1, last, dot(datt_ref[at, last], w8_ref[lag, last, last], 1, 1)),
            (2, first, dot(k_ref[at, first], s8_ref[lag, first, first]) * (scale * 0.5)),
            (2, last, dot(k_ref[at, :], s8_ref[lag, :, last]) * (scale * 0.5)),
            (3, first, dot(q_ref[at, :], s8_ref[lag, first, :], 1, 1)),
            (3, last, dot(q_ref[at, last], s8_ref[lag, last, last], 1, 1)),
        ):
            to = pl.ds(kind * features + h * size, size)
            delayed = pl.ds(pl.multiple_of(kind * features + h * size + zero * 8, 8), size)
            dp_ref[to, lanes] = (grad * slope_ref[delayed, lanes]).astype(BF16)

    total, along = none, none
    for at in chunks:
        grad = (dot(w_ref[at, :], dp_ref[...]) * 0.5).astype(BF16).astype(F32)
        gate_ref[at, :] = grad
        total = total + fold(grad)
        along = along + fold(grad * n_ref[at, :])
    total, along = mean(total, features), mean(along, features)
    place = pick.T

    def leaving(i):
        span = pl.ds(i * per * m, per * m)
        return pltpu.make_async_copy(out_ref.at[span, :], out_hbm.at[span, :], out_sem.at[i])

    for i, at in enumerate(chunks):
        back = inv * (gate_ref[at, :] - total - n_ref[at, :] * along)
        back = back.astype(BF16).astype(F32) + g_ref[at, :].astype(F32)
        y = dot(y_ref[at, :], place).astype(BF16)
        d = dot(back.astype(BF16), place).astype(BF16)
        for j in range(per):
            own = slice(j * c, (j + 1) * c)
            out_ref[pl.ds((i * per + j) * m, m), :] = to_blocks(y[own], d[own])
        leaving(i).start()
    for i in range(len(chunks)):
        leaving(i).wait()


def vmem(n):
    return [pl.BlockSpec(memory_space=pltpu.VMEM)] * n


def smem():
    return pl.BlockSpec(memory_space=pltpu.SMEM)


def hbm(n):
    return [pl.BlockSpec(memory_space=pltpu.HBM)] * n


def grant(room, flags=None):
    return pltpu.CompilerParams(vmem_limit_bytes=(65472 - room) << 10, flags=flags)


def inverse(plan):
    n = plan.shape[-1]
    index = jnp.arange(n, dtype=jnp.int32)
    hit = plan[..., :, None] == index
    return jnp.sum(jnp.where(hit, index[:, None], 0), axis=-2)


def send(plan, x, g):
    tables, peers = plan.shape
    columns = x.shape[0]
    sent = (tables * peers * HALF, 4 * columns)
    return pl.pallas_call(
        send_kernel,
        out_shape=jax.ShapeDtypeStruct(sent, BF16),
        in_specs=vmem(3),
        out_specs=hbm(1)[0],
        scratch_shapes=[pltpu.VMEM(sent, BF16), pltpu.SemaphoreType.DMA((PIECES,))],
        name="send", compiler_params=grant(GS),
    )(plan, x, g)


def home(back, got, columns):
    tables, peers = back.shape
    shape = (columns, tables * peers * TILE)
    return pl.pallas_call(
        home_kernel,
        out_shape=(jax.ShapeDtypeStruct(shape, BF16),) * 2,
        in_specs=vmem(2),
        out_specs=tuple(hbm(2)),
        scratch_shapes=[
            pltpu.VMEM(shape, BF16), pltpu.VMEM(shape, BF16),
            pltpu.SemaphoreType.DMA((2, PIECES)),
        ],
        name="home", compiler_params=grant(GH),
    )(back, got)


def layer(blocks, lengths, plan, slopes, w, o):
    features = o.shape[0]
    heads = slopes.shape[0]
    rows = plan.shape[1] * TILE
    wide = pltpu.VMEM((features, rows), F32)
    thin = pltpu.VMEM((features, rows), BF16)
    return pl.pallas_call(
        layer_kernel,
        out_shape=jax.ShapeDtypeStruct(blocks.shape, BF16),
        in_specs=[smem(), smem()] + vmem(3) + hbm(1),
        out_specs=hbm(1)[0],
        scratch_shapes=[
            pltpu.VMEM((rows, rows), F32), thin, thin, wide, pltpu.VMEM((4 * features, rows), F32), wide, thin, thin, thin,
            pltpu.VMEM((heads, rows, rows), BF16), pltpu.VMEM((heads, rows, rows), F32),
            wide, pltpu.VMEM((heads, rows, rows), BF16), thin, pltpu.VMEM((4 * features, rows), BF16), thin, thin,
            pltpu.VMEM(w.shape[::-1], BF16), pltpu.VMEM(o.shape, BF16), pltpu.VMEM(o.shape, BF16),
            pltpu.VMEM(blocks.shape, BF16),
            pltpu.SemaphoreType.DMA, pltpu.SemaphoreType.DMA((features // STEP,)),
        ],
        name="layer", compiler_params=grant(GL, F0S),
    )(slopes, lengths, plan, blocks, w, pltpu.with_memory_space_constraint(o, pltpu.HBM))


def shards(
    embeds, cotangent, send_plan, work_plan, sequence_tiles, slopes, uvqk_weight, out_weight
):
    columns = embeds.shape[1]
    plan = send_plan[0]
    tables, peers = plan.shape

    def exchange(a):
        shape = a.shape
        a = a.reshape(tables * peers, HALF, 4 * columns)
        a = lax.all_to_all(a, ("table", "replica"), split_axis=0, concat_axis=0, tiled=True)
        return a.reshape(shape)

    got = exchange(send(plan, embeds.T, cotangent.T))
    done = layer(got, sequence_tiles[0, 0], work_plan[0], slopes, uvqk_weight, out_weight)
    y, d = home(inverse(plan), exchange(done), columns)
    return y.T, d.T


def solution(mesh):
    in_specs = (
        P("replica", "table"),
        P("replica", "table"),
        P("replica", None, None),
        P("replica", "table", None),
        P("replica", "table", None),
        P(),
        P(),
        P(),
    )
    out_specs = (P("replica", "table"), P("replica", "table"))
    return jax.shard_map(shards, mesh=mesh, in_specs=in_specs, out_specs=out_specs, check_vma=False)
```

```python
import jax
import jax.numpy as jnp
from jax import lax
from jax.experimental import pallas as pl
from jax.experimental.pallas import tpu as pltpu
from jax.sharding import PartitionSpec as P

TILE = 8
HALF = 4
EPSILON = 1e-05
BF16 = jnp.bfloat16
F32 = jnp.float32
FAR = 1e30
STEP = 128
PIECES = 4
GS, GL, GH = 2200, 16000, 50000


def dot(a, b, ca=1, cb=0):
    return lax.dot_general(a, b, (((ca,), (cb,)), ((), ())), preferred_element_type=F32)


def one_hot(rows, target):
    index = lax.broadcasted_iota(jnp.int32, (rows, target.shape[1]), 0)
    return jnp.where(index == target, 1.0, 0.0).astype(BF16)


def spread(plan, repeat):
    slots = plan.shape[1]
    lanes = slots * repeat
    slot = lax.broadcasted_iota(jnp.int32, (slots, lanes), 0)
    lane = lax.broadcasted_iota(jnp.int32, (slots, lanes), 1)
    pick = jnp.where(lane // repeat == slot, 1.0, 0.0).astype(BF16)
    return dot(plan.astype(F32).astype(BF16), pick).astype(jnp.int32)


def spots(plan):
    rows = plan.shape[1] * TILE
    inner = lax.broadcasted_iota(jnp.int32, (1, rows), 1) % TILE
    return spread(plan, TILE) * HALF + inner % HALF + (inner // HALF) * (rows // 2)


def to_blocks(top, bottom):
    m = top.shape[1] // 2
    return jnp.concatenate([top[:, :m], bottom[:, :m], top[:, m:], bottom[:, m:]], axis=0).T


def from_blocks(block):
    turned = block.T
    c2 = turned.shape[0] // 2
    return jnp.concatenate([turned[:c2], turned[c2:]], axis=1)


def send_kernel(plan_ref, x_ref, g_ref, out_hbm, out_ref, moved_ref, out_sem):
    tables, peers = plan_ref.shape
    rows = peers * TILE
    m = peers * HALF
    per = tables // PIECES

    def leaving(i):
        span = pl.ds(i * per * m, per * m)
        return pltpu.make_async_copy(out_ref.at[span, :], out_hbm.at[span, :], out_sem.at[i])

    lane = lax.broadcasted_iota(jnp.int32, (1, m), 1)
    base = spread(plan_ref[...], HALF) * TILE + lane % HALF
    target = jnp.concatenate([base, base + HALF], axis=1)
    for i in range(PIECES):
        for t in range(i * per, (i + 1) * per):
            pick = one_hot(rows, target[t : t + 1])
            span = pl.ds(t * rows, rows)
            both = jnp.concatenate([x_ref[:, span], g_ref[:, span]], axis=0)
            moved_ref[t] = dot(both, pick).astype(BF16)
        for t in range(i * per, (i + 1) * per):
            turned = jnp.concatenate([moved_ref[t, :, :m], moved_ref[t, :, m:]], axis=0).T
            out_ref[pl.ds(t * m, m), :] = turned
        leaving(i).start()
    for i in range(PIECES):
        leaving(i).wait()


def home_kernel(back_ref, in_ref, y_hbm, d_hbm, y_ref, d_ref, out_sem):
    tables, peers = back_ref.shape
    rows = peers * TILE
    m = peers * HALF
    per = tables // PIECES
    target = spots(back_ref[...])
    c = y_ref.shape[0]

    def leaving(i):
        span = pl.ds(i * per * rows, per * rows)
        return [
            pltpu.make_async_copy(src.at[:, span], dst.at[:, span], out_sem.at[j, i])
            for j, (src, dst) in enumerate(((y_ref, y_hbm), (d_ref, d_hbm)))
        ]

    for i in range(PIECES):
        for t in range(i * per, (i + 1) * per):
            place = one_hot(2 * m, target[t : t + 1])
            span = pl.ds(t * rows, rows)
            got = dot(from_blocks(in_ref[pl.ds(t * m, m), :]), place).astype(BF16)
            y_ref[:, span] = got[:c]
            d_ref[:, span] = got[c:]
        for copy in leaving(i):
            copy.start()
    for i in range(PIECES):
        for copy in leaving(i):
            copy.wait()


def fold(x):
    return jnp.sum(x.reshape(x.shape[0] // 8, 8, x.shape[1]), axis=0)


def mean(partial, n):
    return jnp.sum(partial, axis=0, keepdims=True) * (1.0 / n)


def allowed(lengths_ref, rows):
    key = lax.broadcasted_iota(jnp.int32, (rows, rows // 2), 0)
    ask = lax.broadcasted_iota(jnp.int32, (1, rows), 1)
    key_of, ask_of, bound = jnp.zeros_like(key), jnp.zeros_like(ask), 0
    for j in range(lengths_ref.shape[0] - 1):
        bound = bound + lengths_ref[j] * TILE
        key_of = jnp.where(key >= bound, j + 1, key_of)
        ask_of = jnp.where(ask >= bound, j + 1, ask_of)
    key, key_of = (jnp.concatenate([a, a], axis=1) for a in (key, key_of))
    return jnp.where((key <= ask) & (key_of == ask_of), 0.0, FAR)


def activate(half):
    lift = 1.0 + jnp.tanh(half)
    act = half * lift
    return act, lift * (((half + half) - act) + 1.0)


def layer_kernel(
    slopes_ref, lengths_ref, plan_ref, in_ref, w_ref, o_hbm, out_hbm,
    far_ref, x_ref, g_ref, n_ref, slope_ref, gate_ref, v_ref, q_ref, k_ref, w8_ref, d8_ref, att_ref,
    s8_ref, datt_ref, dp_ref, y_ref, dx_ref, wt_ref, ot_ref, o_ref, out_ref, in_sem, out_sem,
):
    features, rows = x_ref.shape
    heads = slopes_ref.shape[0]
    size = features // heads
    m = rows // 2
    tables = in_ref.shape[0] // m
    c = features // tables
    per = STEP // c
    chunks = [pl.ds(part, STEP) for part in range(0, features, STEP)]
    none = jnp.zeros((8, rows), F32)
    first, last = pl.ds(0, m), pl.ds(m, m)
    zero = jnp.minimum(lengths_ref[0], 0)
    read = pltpu.make_async_copy(o_hbm, o_ref, in_sem)
    read.start()

    for t in range(tables):
        both = from_blocks(in_ref[pl.ds(t * m, m), :])
        x_ref[pl.ds(t * c, c), :] = both[:c]
        g_ref[pl.ds(t * c, c), :] = both[c:]
    pick = one_hot(rows, spots(plan_ref[...]))
    far_ref[...] = allowed(lengths_ref, rows)
    total = none
    for at in chunks:
        x = dot(x_ref[at, :], pick)
        x_ref[at, :] = x.astype(BF16)
        n_ref[at, :] = x
        total = total + fold(x)
        g_ref[at, :] = dot(g_ref[at, :], pick).astype(BF16)
    centre = mean(total, features)
    total = none
    for at in chunks:
        x = n_ref[at, :] - centre
        total = total + fold(x * x)
    inv = lax.rsqrt(mean(total, features) + EPSILON)
    for at in chunks:
        normed = (n_ref[at, :] - centre) * inv
        n_ref[at, :] = normed
        dx_ref[at, :] = (normed * 0.5).astype(BF16)

    scale = size ** (-0.5)
    for part in range(0, 4 * features, STEP):
        wt_ref[pl.ds(part, STEP), :] = w_ref[:, pl.ds(part, STEP)].T
    for part in range(0, 4 * features, STEP):
        half = dot(wt_ref[pl.ds(part, STEP), :], dx_ref[...])
        act, slope_ref[pl.ds(part, STEP), :] = activate(half)
        at = pl.ds(part % features, STEP)
        kind = part // features
        if kind == 0:
            gate_ref[at, :] = act
        elif kind == 1:
            v_ref[at, :] = act.astype(BF16)
        elif kind == 2:
            q_ref[at, :] = (act * (scale * 0.5)).astype(BF16)
        else:
            k_ref[at, :] = act.astype(BF16)

    row = lax.broadcasted_iota(jnp.int32, (m, rows), 0)
    col = lax.broadcasted_iota(jnp.int32, (m, rows), 1)
    apart = (col - row).astype(F32)
    for h in range(heads):
        at = pl.ds(h * size, size)
        slope = slopes_ref[h] * 0.5
        for b in range(2):
            keys = pl.ds(b * m, m)
            asks = pl.ds(b * m, rows - b * m)
            dist = apart[:, : rows - b * m]
            half = dot(k_ref[at, keys], q_ref[at, asks], 0, 0)
            half = (half - far_ref[keys, asks]) - slope * dist
            act, d8_ref[h, keys, asks] = activate(half)
            w8_ref[h, keys, asks] = act.astype(BF16)
    for h in range(heads):
        at = pl.ds(h * size, size)
        att_ref[at, pl.ds(0, m)] = dot(v_ref[at, pl.ds(0, m)], w8_ref[h, pl.ds(0, m), pl.ds(0, m)])
        att_ref[at, pl.ds(m, m)] = dot(v_ref[at, :], w8_ref[h, :, pl.ds(m, m)])

    read.wait()
    for at in chunks:
        ot_ref[at, :] = o_ref[:, at].T
    total = none
    for at in chunks:
        total = total + fold(att_ref[at, :])
    centre = mean(total, features)
    total = none
    for at in chunks:
        x = att_ref[at, :] - centre
        total = total + fold(x * x)
    inv_a = lax.rsqrt(mean(total, features) + EPSILON)
    total, along = none, none
    for at in chunks:
        even = (att_ref[at, :] - centre) * inv_a
        att_ref[at, :] = even
        gate = gate_ref[at, :]
        datt_ref[at, :] = (even * gate).astype(BF16)
        d_gated = dot(o_ref[at, :], g_ref[...]).astype(BF16).astype(F32)
        dp_ref[at, :] = (d_gated * even * slope_ref[at, :]).astype(BF16)
        grad = d_gated * gate
        gate_ref[at, :] = grad
        total = total + fold(grad)
        along = along + fold(grad * even)
    for at in chunks:
        y_ref[at, :] = (x_ref[at, :].astype(F32) + dot(ot_ref[at, :], datt_ref[...])).astype(BF16)
    total, along = mean(total, features), mean(along, features)
    for at in chunks:
        grad = inv_a * (gate_ref[at, :] - total - att_ref[at, :] * along)
        datt_ref[at, :] = grad.astype(BF16)

    for h in range(heads):
        at = pl.ds(h * size, size)
        top = dot(v_ref[at, first], datt_ref[at, :], 0, 0) * d8_ref[h + zero, first, :]
        s8_ref[h, first, :] = top.astype(BF16)
        low = dot(v_ref[at, last], datt_ref[at, last], 0, 0) * d8_ref[h + zero, last, last]
        s8_ref[h, last, last] = low.astype(BF16)
    for h in range(heads):
        at = pl.ds(h * size, size)
        lag = h + 0
        for kind, lanes, grad in (
            (1, first, dot(datt_ref[at, :], w8_ref[lag, first, :], 1, 1)),
            (1, last, dot(datt_ref[at, last], w8_ref[lag, last, last], 1, 1)),
            (2, first, dot(k_ref[at, first], s8_ref[lag, first, first]) * (scale * 0.5)),
            (2, last, dot(k_ref[at, :], s8_ref[lag, :, last]) * (scale * 0.5)),
            (3, first, dot(q_ref[at, :], s8_ref[lag, first, :], 1, 1)),
            (3, last, dot(q_ref[at, last], s8_ref[lag, last, last], 1, 1)),
        ):
            to = pl.ds(kind * features + h * size, size)
            delayed = pl.ds(pl.multiple_of(kind * features + h * size + zero * 8, 8), size)
            dp_ref[to, lanes] = (grad * slope_ref[delayed, lanes]).astype(BF16)

    total, along = none, none
    for at in (pl.ds(0, 2 * STEP), pl.ds(2 * STEP, 2 * STEP)):
        gate_ref[at, :] = (dot(w_ref[at, :], dp_ref[...]) * 0.5).astype(BF16).astype(F32)
    for at in chunks:
        grad = gate_ref[at, :]
        total = total + fold(grad)
        along = along + fold(grad * n_ref[at, :])
    total, along = mean(total, features), mean(along, features)
    place = pick.T

    def leaving(i):
        span = pl.ds(i * per * m, per * m)
        return pltpu.make_async_copy(out_ref.at[span, :], out_hbm.at[span, :], out_sem.at[i])

    for at in chunks:
        back = inv * (gate_ref[at, :] - total - n_ref[at, :] * along)
        back = back.astype(BF16).astype(F32) + g_ref[at, :].astype(F32)
        datt_ref[at, :] = back.astype(BF16)
    y_ref[...] = dot(y_ref[...], place).astype(BF16)
    datt_ref[...] = dot(datt_ref[...], place).astype(BF16)
    for i in range(len(chunks)):
        for t in range(i * per, (i + 1) * per):
            own = pl.ds(t * c, c)
            out_ref[pl.ds(t * m, m), :] = to_blocks(y_ref[own, :], datt_ref[own, :])
        leaving(i).start()
    for i in range(len(chunks)):
        leaving(i).wait()


def vmem(n):
    return [pl.BlockSpec(memory_space=pltpu.VMEM)] * n


def smem():
    return pl.BlockSpec(memory_space=pltpu.SMEM)


def hbm(n):
    return [pl.BlockSpec(memory_space=pltpu.HBM)] * n


def grant(room):
    return pltpu.CompilerParams(vmem_limit_bytes=(65472 - room) << 10)


def inverse(plan):
    n = plan.shape[-1]
    index = jnp.arange(n, dtype=jnp.int32)
    hit = plan[..., :, None] == index
    return jnp.sum(jnp.where(hit, index[:, None], 0), axis=-2)


def send(plan, x, g):
    tables, peers = plan.shape
    columns = x.shape[0]
    sent = (tables * peers * HALF, 4 * columns)
    return pl.pallas_call(
        send_kernel,
        out_shape=jax.ShapeDtypeStruct(sent, BF16),
        in_specs=vmem(3),
        out_specs=hbm(1)[0],
        scratch_shapes=[
            pltpu.VMEM(sent, BF16), pltpu.VMEM((tables, 2 * columns, peers * TILE), BF16),
            pltpu.SemaphoreType.DMA((PIECES,)),
        ],
        name="send", compiler_params=grant(GS),
    )(plan, x, g)


def home(back, got, columns):
    tables, peers = back.shape
    shape = (columns, tables * peers * TILE)
    return pl.pallas_call(
        home_kernel,
        out_shape=(jax.ShapeDtypeStruct(shape, BF16),) * 2,
        in_specs=vmem(2),
        out_specs=tuple(hbm(2)),
        scratch_shapes=[
            pltpu.VMEM(shape, BF16), pltpu.VMEM(shape, BF16),
            pltpu.SemaphoreType.DMA((2, PIECES)),
        ],
        name="home", compiler_params=grant(GH),
    )(back, got)


def layer(blocks, lengths, plan, slopes, w, o):
    features = o.shape[0]
    heads = slopes.shape[0]
    rows = plan.shape[1] * TILE
    wide = pltpu.VMEM((features, rows), F32)
    thin = pltpu.VMEM((features, rows), BF16)
    return pl.pallas_call(
        layer_kernel,
        out_shape=jax.ShapeDtypeStruct(blocks.shape, BF16),
        in_specs=[smem(), smem()] + vmem(3) + hbm(1),
        out_specs=hbm(1)[0],
        scratch_shapes=[
            pltpu.VMEM((rows, rows), F32), thin, thin, wide, pltpu.VMEM((4 * features, rows), F32), wide, thin, thin, thin,
            pltpu.VMEM((heads, rows, rows), BF16), pltpu.VMEM((heads, rows, rows), F32),
            wide, pltpu.VMEM((heads, rows, rows), BF16), thin, pltpu.VMEM((4 * features, rows), BF16), thin, thin,
            pltpu.VMEM(w.shape[::-1], BF16), pltpu.VMEM(o.shape, BF16), pltpu.VMEM(o.shape, BF16),
            pltpu.VMEM(blocks.shape, BF16),
            pltpu.SemaphoreType.DMA, pltpu.SemaphoreType.DMA((features // STEP,)),
        ],
        name="layer", compiler_params=grant(GL),
    )(slopes, lengths, plan, blocks, w, pltpu.with_memory_space_constraint(o, pltpu.HBM))


def shards(
    embeds, cotangent, send_plan, work_plan, sequence_tiles, slopes, uvqk_weight, out_weight
):
    columns = embeds.shape[1]
    plan = send_plan[0]
    tables, peers = plan.shape

    def exchange(a):
        shape = a.shape
        a = a.reshape(tables * peers, HALF, 4 * columns)
        a = lax.all_to_all(a, ("table", "replica"), split_axis=0, concat_axis=0, tiled=True)
        return a.reshape(shape)

    got = exchange(send(plan, embeds.T, cotangent.T))
    done = layer(got, sequence_tiles[0, 0], work_plan[0], slopes, uvqk_weight, out_weight)
    y, d = home(inverse(plan), exchange(done), columns)
    return y.T, d.T


def solution(mesh):
    in_specs = (
        P("replica", "table"),
        P("replica", "table"),
        P("replica", None, None),
        P("replica", "table", None),
        P("replica", "table", None),
        P(),
        P(),
        P(),
    )
    out_specs = (P("replica", "table"), P("replica", "table"))
    return jax.shard_map(shards, mesh=mesh, in_specs=in_specs, out_specs=out_specs, check_vma=False)
```
